32 devices in a mesh: prefix: 16 (over z, x, core), tensor: 2 (over y).
Axes of the slice: x: 2, y: 2, z: 4, core: 2. Of those that a mesh axis runs over, the one named last changes fastest.
Arguments:
- queries: bfloat16 [1024, 8192], P(('prefix', 'tensor')), may hold values from -24 to 24
- suffix_kv: bfloat16 [1024, 2, 8, 64, 128], P('prefix', None, 'tensor'), may hold values from -15 to 15
- suffix_lengths: int32 [1024], P('prefix'), may hold values from 1 to 64
- prefix_kv: bfloat16 [16, 2, 8, 4096, 128], P('prefix', None, 'tensor'), may hold values from -16 to 16
- tree_ids: int32 [1024], P('prefix'), may hold values from 0 to 15, as said below
- owner_map: int32 [16], replicated, may hold values from 0 to 15, as said below
Outputs:
- attended: bfloat16 [1024, 8192], P(('prefix', 'tensor'))
The draws below stay inside these ranges and needn't reach their ends.
Inputs may be any that keep to these rules, and one draw needn't show every extreme that they name: `tree_ids`: in each aligned block of 64 rows (the rows of one index of prefix) no prompt is named by more than 8 rows, and some prompt is named by exactly 8 rows in every block. `owner_map`: A permutation: every row of prefix_kv holds the prefix of exactly one prompt.
All inputs are finite; a program needn't handle non-finite values.
Results may differ from the reference program's by a relative error of at most 0.0017.
Values may be sent and summed in bfloat16 or wider, within the bound.
A program may use at most 64 MiB of HBM per device.

```python
import math
import jax
import jax.numpy as jnp
from jax import lax

H = 64
KVH = 8
HD = 128
PLEN = 4096
SUF = 64
ROWS_DEV = 64
PREFIXES = 16
ROWS = 1024
MOST = 8


def tree_layout(key):
    base_key = jax.random.fold_in(key, 101)
    hot_key, pick_key = jax.random.split(base_key)
    candidates = PREFIXES * MOST
    cand_prompt = jnp.arange(candidates, dtype=jnp.int32) // MOST
    hottest = jax.random.randint(hot_key, (), 0, PREFIXES, dtype=jnp.int32)
    popular = (cand_prompt * 5 + hottest) % 4 == 0

    def one_block(block_key):
        order_key, shuffle_key = jax.random.split(block_key)
        ranking = jax.random.permutation(order_key, candidates).astype(jnp.int32)
        ranking = ranking - jnp.where(popular, candidates, 0) - jnp.where(cand_prompt == hottest, 2 * candidates, 0)
        chosen = jnp.argsort(ranking, stable=True)[:ROWS_DEV]
        return jax.random.permutation(shuffle_key, cand_prompt[chosen])
    layout = jax.vmap(one_block)(jax.random.split(pick_key, PREFIXES))
    return layout.reshape(-1).astype(jnp.int32)


def owner_layout(key):
    return jax.random.permutation(jax.random.fold_in(key, 202), PREFIXES).astype(jnp.int32)


def draw_tree_ids(key, part):
    return tree_layout(key)


def draw_owner_map(key, part):
    return owner_layout(key)


def draw_queries(key, part):
    base_key = jax.random.fold_in(key, 505)
    drawn = jax.random.normal(base_key, (ROWS, H * HD), jnp.float32)
    return jnp.clip(drawn, -6.0, 6.0).astype(jnp.bfloat16)


def draw_prefix_kv(key, part):
    base_key = jax.random.fold_in(key, 606)
    shape = (PREFIXES, 2, KVH, PLEN, HD)
    drawn = 0.6 * jax.random.normal(base_key, shape, jnp.float32)
    return jnp.clip(drawn, -3.6, 3.6).astype(jnp.bfloat16)


def with_ends(result, stream_key, low, top_value):
    index_at = [jax.random.randint(jax.random.fold_in(stream_key, axis), (), 0, length) for axis, length in enumerate(result.shape)]
    longest = result.shape.index(max(result.shape))
    beside = index_at[:longest] + [(index_at[longest] + 1) % result.shape[longest]] + index_at[longest + 1:]
    return result.at[tuple(index_at)].set(low).at[tuple(beside)].set(top_value)


def shard_levels(own_key, dims, shards, least, high):
    level = 1.0
    for dim, parts in shards:
        steps = jax.random.uniform(jax.random.fold_in(jax.random.fold_in(own_key, 6), dim), (parts,), jnp.float32, least / len(shards), high / len(shards))
        level = level * jnp.repeat(jnp.exp(steps), dims[dim] // parts).reshape((-1,) + (1,) * (len(dims) - 1 - dim))
    return level


def noise(stream_key, dims, deviation, bound, cuts=(), kind=jnp.bfloat16):
    values = jax.random.normal(stream_key, dims, jnp.float32) * deviation
    if len(cuts) > 0:
        values = shard_levels(stream_key, dims, cuts, -0.22, 0.18) * values
    return jnp.clip(values, min=-bound, max=bound).astype(kind)


def setup_inputs(seed: int = 0) -> dict:
    key_list = jax.random.split(jax.random.key(seed), 7)
    return {
        "queries": draw_queries(jax.random.fold_in(key_list[6], 71), 0),
        "suffix_kv": noise(key_list[1], (ROWS, 2, KVH, SUF, HD), 2.5, 15.0, ((0, 16), (2, 2))),
        "suffix_lengths": with_ends(jax.random.randint(key_list[2], (ROWS,), 1, SUF + 1), jax.random.fold_in(key_list[2], 1), 1, SUF).astype(jnp.int32),
        "prefix_kv": draw_prefix_kv(jax.random.fold_in(key_list[6], 71), 0),
        "tree_ids": draw_tree_ids(jax.random.fold_in(key_list[6], 71), 0),
        "owner_map": draw_owner_map(jax.random.fold_in(key_list[6], 71), 0),
    }


def rounded_f32(weights):
    return lax.optimization_barrier(weights.astype(jnp.bfloat16)).astype(jnp.float32)

def suffix_block(packed):
    query_rows, cache_rows, length_rows = packed
    score_scale = 1.0 / math.sqrt(HD)
    cache_f32 = cache_rows.astype(jnp.float32)
    suffix_scores = jnp.einsum('rgid,rgnd->rgin', query_rows, cache_f32[:, 0]) * score_scale
    position = jnp.arange(SUF, dtype=jnp.int32)
    is_live = (position[None, :] < length_rows[:, None])[:, None, None, :]
    suffix_top = lax.optimization_barrier(jnp.max(jnp.where(is_live, suffix_scores, -jnp.inf), axis=-1))
    suffix_weights = jnp.where(is_live, jnp.exp(suffix_scores - suffix_top[..., None]), 0.0)
    suffix_total = lax.optimization_barrier(jnp.sum(suffix_weights, axis=-1))
    suffix_sum = jnp.einsum('rgin,rgnd->rgid', rounded_f32(suffix_weights), cache_f32[:, 1])
    return (suffix_top, suffix_total, suffix_sum)

def reference(queries, suffix_kv, suffix_lengths, prefix_kv, tree_ids, owner_map):
    group_size = H // KVH
    score_scale = 1.0 / math.sqrt(HD)
    query_f32 = queries.astype(jnp.float32).reshape(ROWS, KVH, group_size, HD)
    stored = jnp.take(owner_map, tree_ids).astype(jnp.int32)
    capacity = PREFIXES * MOST

    def one_prefix(running, stored_index):
        part_all, top_all, total_all = running
        picked = jnp.argsort((stored != stored_index).astype(jnp.int32), stable=True)[:capacity].astype(jnp.int32)
        is_valid = stored[picked] == stored_index
        prefix_f32 = lax.dynamic_index_in_dim(prefix_kv, stored_index, 0, keepdims=False).astype(jnp.float32)
        chosen = query_f32[picked]
        scores = jnp.einsum('rgid,gnd->rgin', chosen, prefix_f32[0]) * score_scale
        row_top = lax.optimization_barrier(jnp.max(scores, axis=-1))
        weights = jnp.exp(scores - row_top[..., None])
        mass_sum = lax.optimization_barrier(jnp.sum(weights, axis=-1))
        prefix_part = jnp.einsum('rgin,gnd->rgid', rounded_f32(weights), prefix_f32[1]) / mass_sum[..., None]
        keep_rows = is_valid[:, None, None]
        part_all = part_all.at[picked].add(jnp.where(keep_rows[..., None], prefix_part, 0.0))
        top_all = top_all.at[picked].add(jnp.where(keep_rows, row_top, 0.0))
        total_all = total_all.at[picked].add(jnp.where(keep_rows, mass_sum, 0.0))
        return ((part_all, top_all, total_all), None)
    starting = (jnp.zeros((ROWS, KVH, group_size, HD), jnp.float32), jnp.zeros((ROWS, KVH, group_size), jnp.float32), jnp.zeros((ROWS, KVH, group_size), jnp.float32))
    (prefix_part, prefix_top, prefix_total), unused = lax.scan(one_prefix, starting, jnp.arange(PREFIXES, dtype=jnp.int32))
    blocks = ROWS // ROWS_DEV
    suffix_top, suffix_total, suffix_sum = lax.map(suffix_block, (query_f32.reshape(blocks, ROWS_DEV, KVH, group_size, HD), suffix_kv.reshape(blocks, ROWS_DEV, 2, KVH, SUF, HD), suffix_lengths.reshape(blocks, ROWS_DEV)))
    suffix_top = suffix_top.reshape(ROWS, KVH, group_size)
    suffix_total = suffix_total.reshape(ROWS, KVH, group_size)
    suffix_sum = suffix_sum.reshape(ROWS, KVH, group_size, HD)
    joint_top = jnp.maximum(prefix_top, suffix_top)
    prefix_mass = prefix_total * jnp.exp(prefix_top - joint_top)
    suffix_mass = jnp.exp(suffix_top - joint_top)
    attended = (prefix_mass[..., None] * prefix_part + suffix_mass[..., None] * suffix_sum) / (prefix_mass + suffix_mass * suffix_total)[..., None]
    return attended.reshape(ROWS, H * HD).astype(jnp.bfloat16)
```

```python
import math

import jax
import jax.numpy as jnp
from jax import lax
from jax.experimental import pallas as pl
from jax.experimental.pallas import tpu as pltpu
from jax.sharding import PartitionSpec as P

H = 64
KVH = 8
HD = 128
LANES = 128
GROUP = H // KVH
LOG2E = 1.4426950408889634
SCALE2 = LOG2E / math.sqrt(HD)


def nt_dot(a, b):
    return lax.dot_general(a, b, (((1,), (1,)), ((), ())), preferred_element_type=jnp.float32)


def nn_dot(a, b):
    return lax.dot_general(a, b, (((1,), (0,)), ((), ())), preferred_element_type=jnp.float32)


def prefix_kernel(q_ref, kv_ref, out_ref, lse_ref):
    g = pl.program_id(0)
    slots = q_ref.shape[0]
    length = kv_ref.shape[3]
    chunk = min(1024, length)
    pair = 2
    lane = lax.broadcasted_iota(jnp.int32, (slots, LANES), 1)

    @pl.when(g == 0)
    def _():
        lse_ref[...] = jnp.zeros_like(lse_ref)

    def one_tile(t, carry):
        cols = [pl.ds(pl.multiple_of((t * pair + i) * HD, HD), HD) for i in range(pair)]
        q = jnp.concatenate([q_ref[:, c] for c in cols], axis=0)
        top = total = acc = None
        for start in range(0, length, chunk):
            s = nt_dot(q, kv_ref[0, 0, 0, start : start + chunk, :]) * SCALE2
            here = jnp.max(s, axis=1, keepdims=True)
            new_top = here if top is None else jnp.maximum(top, here)
            w = jnp.exp2(s - new_top)
            w_sum = jnp.sum(w, axis=1, keepdims=True)
            w_v = nn_dot(w.astype(jnp.bfloat16), kv_ref[0, 1, 0, start : start + chunk, :])
            if top is None:
                total, acc = w_sum, w_v
            else:
                fade = jnp.exp2(top - new_top)
                total = total * fade + w_sum
                acc = acc * fade + w_v
            top = new_top
        part = (acc / total).astype(jnp.bfloat16)
        lse = top + jnp.log(total) * LOG2E
        for i in range(pair):
            rows = slice(i * slots, (i + 1) * slots)
            out_ref[:, cols[i]] = part[rows]
            head = g * GROUP + t * pair + i
            lse_ref[...] = jnp.where(lane == head, lse[rows], lse_ref[...])
        return carry

    lax.fori_loop(0, GROUP // pair, one_tile, 0)


def prefix_attend(slot_rows, prefix_kv):
    slots, row_width = slot_rows.shape
    kv_heads, length = prefix_kv.shape[2], prefix_kv.shape[3]
    wide = GROUP * HD
    return pl.pallas_call(
        prefix_kernel,
        grid=(kv_heads,),
        out_shape=(
            jax.ShapeDtypeStruct((slots, row_width), jnp.bfloat16),
            jax.ShapeDtypeStruct((slots, LANES), jnp.float32),
        ),
        in_specs=[
            pl.BlockSpec((slots, wide), lambda g: (0, g)),
            pl.BlockSpec((1, 2, 1, length, HD), lambda g: (0, 0, g, 0, 0)),
        ],
        out_specs=(
            pl.BlockSpec((slots, wide), lambda g: (0, g)),
            pl.BlockSpec((slots, LANES), lambda g: (0, 0)),
        ),
        compiler_params=pltpu.CompilerParams(vmem_limit_bytes=40 << 20),
        cost_estimate=pl.CostEstimate(
            flops=4 * slots * row_width * length,
            bytes_accessed=4 * kv_heads * length * HD + 4 * slots * row_width,
            transcendentals=slots * row_width // HD * length,
        ),
        name="prefix_attend",
    )(slot_rows, prefix_kv)


def suffix_kernel(q_ref, kv_ref, len_ref, sum_ref, lse_ref):
    rows, kv_heads, count = kv_ref.shape[0], kv_ref.shape[2], kv_ref.shape[3]
    tall = GROUP * rows
    row_of = lax.broadcasted_iota(jnp.int32, (tall, rows * count), 0) % rows
    col = lax.broadcasted_iota(jnp.int32, (tall, rows * count), 1)
    lengths = jnp.concatenate([len_ref[:, 0:1]] * GROUP, axis=0)
    live = (col // count == row_of) & (col % count < lengths)
    lane = lax.broadcasted_iota(jnp.int32, (rows, LANES), 1)
    lse_all = jnp.zeros((rows, LANES), jnp.float32)
    for g in range(kv_heads):
        heads = range(g * GROUP, (g + 1) * GROUP)
        q = jnp.concatenate([q_ref[:, h * HD : (h + 1) * HD] for h in heads], axis=0)
        keys = kv_ref[:, 0, g].reshape(rows * count, HD)
        values = kv_ref[:, 1, g].reshape(rows * count, HD)
        s = jnp.where(live, nt_dot(q, keys) * SCALE2, -jnp.inf)
        top = jnp.max(s, axis=1, keepdims=True)
        w = jnp.exp2(s - top)
        total = jnp.sum(w, axis=1, keepdims=True)
        part = nn_dot(w.astype(jnp.bfloat16), values) / total
        lse = top + jnp.log(total) * LOG2E
        for i, h in enumerate(heads):
            sum_ref[:, h * HD : (h + 1) * HD] = part[i * rows : (i + 1) * rows]
            lse_all = jnp.where(lane == h, lse[i * rows : (i + 1) * rows], lse_all)
    lse_ref[...] = lse_all


def suffix_attend(local_q, suffix_kv, lengths):
    rows_home, row_width = local_q.shape
    kv_heads, count = suffix_kv.shape[2], suffix_kv.shape[3]
    rows = math.gcd(rows_home, 16)
    wide_lengths = jnp.broadcast_to(lengths[:, None], (rows_home, LANES))
    return pl.pallas_call(
        suffix_kernel,
        grid=(rows_home // rows,),
        out_shape=(
            jax.ShapeDtypeStruct((rows_home, row_width), jnp.float32),
            jax.ShapeDtypeStruct((rows_home, LANES), jnp.float32),
        ),
        in_specs=[
            pl.BlockSpec((rows, row_width), lambda b: (b, 0)),
            pl.BlockSpec((rows, 2, kv_heads, count, HD), lambda b: (b, 0, 0, 0, 0)),
            pl.BlockSpec((rows, LANES), lambda b: (b, 0)),
        ],
        out_specs=(
            pl.BlockSpec((rows, row_width), lambda b: (b, 0)),
            pl.BlockSpec((rows, LANES), lambda b: (b, 0)),
        ),
        compiler_params=pltpu.CompilerParams(vmem_limit_bytes=40 << 20),
        cost_estimate=pl.CostEstimate(
            flops=4 * rows_home * row_width * count * rows,
            bytes_accessed=4 * rows_home * kv_heads * count * HD + 6 * rows_home * row_width,
            transcendentals=rows_home * row_width // HD * count * rows,
        ),
        name="suffix_attend",
    )(local_q, suffix_kv, wide_lengths)


def merge_kernel(pick_ref, back_ref, sum_ref, lse_ref, out_ref):
    row_width = out_ref.shape[1]
    heads = row_width // HD
    pick = pick_ref[...]
    prefix_lse = nn_dot(pick, back_ref[:, row_width : row_width + LANES])
    for i in range(1, 3):
        left = row_width + i * LANES
        prefix_lse = prefix_lse + nn_dot(pick, back_ref[:, left : left + LANES])
    suffix_lse = lse_ref[...]
    joint = jnp.maximum(prefix_lse, suffix_lse)
    prefix_mass = jnp.exp2(prefix_lse - joint)
    suffix_mass = jnp.exp2(suffix_lse - joint)
    mass = prefix_mass + suffix_mass
    prefix_share = prefix_mass / mass
    suffix_share = suffix_mass / mass
    for h in range(heads):
        cols = slice(h * HD, (h + 1) * HD)
        part = nn_dot(pick, back_ref[:, cols])
        mixed = prefix_share[:, h : h + 1] * part + suffix_share[:, h : h + 1] * sum_ref[:, cols]
        out_ref[:, cols] = mixed.astype(jnp.bfloat16)


def merge(pick, back, suffix_sum, suffix_lse):
    rows_home, row_width = suffix_sum.shape
    return pl.pallas_call(
        merge_kernel,
        out_shape=jax.ShapeDtypeStruct((rows_home, row_width), jnp.bfloat16),
        name="merge",
    )(pick, back, suffix_sum, suffix_lse)


def split_three(x):
    high = lax.reduce_precision(x, 8, 7)
    rest = x - high
    middle = lax.reduce_precision(rest, 8, 7)
    low = rest - middle
    return [piece.astype(jnp.bfloat16) for piece in (high, middle, low)]


def on_device(queries, suffix_kv, suffix_lengths, prefix_kv, tree_ids, owner_map):
    owners = lax.axis_size("prefix")
    local_q = lax.all_to_all(queries, "tensor", split_axis=1, concat_axis=0, tiled=True)
    rows_home, row_width = local_q.shape
    capacity = max(2, 2 * rows_home // owners)
    slots = owners * capacity
    prompts = owner_map.shape[0]
    prompt_iota = jnp.arange(prompts, dtype=jnp.int32)
    prompt_match = tree_ids[:, None] == prompt_iota[None, :]
    owner_row = jnp.sum(jnp.where(prompt_match, owner_map[None, :], 0), axis=1)
    row_iota = jnp.arange(rows_home, dtype=jnp.int32)
    earlier = (tree_ids[:, None] == tree_ids[None, :]) & (row_iota[None, :] < row_iota[:, None])
    slot_rank = jnp.sum(earlier.astype(jnp.int32), axis=1)
    slot_of = owner_row * capacity + slot_rank
    slot_iota = jnp.arange(slots, dtype=jnp.int32)
    pick = (slot_of[:, None] == slot_iota[None, :]).astype(jnp.bfloat16)
    outgoing = lax.dot_general(
        pick, local_q, (((0,), (0,)), ((), ())), preferred_element_type=jnp.float32
    ).astype(jnp.bfloat16)
    arrived = lax.all_to_all(
        outgoing.reshape(owners, capacity, row_width),
        "prefix",
        split_axis=0,
        concat_axis=0,
        tiled=True,
    ).reshape(slots, row_width)
    suffix_sum, suffix_lse = suffix_attend(local_q, suffix_kv, suffix_lengths)
    part, lse = prefix_attend(arrived, prefix_kv)
    packed = jnp.concatenate([part] + split_three(lse), axis=1)
    back = lax.all_to_all(
        packed.reshape(owners, capacity, packed.shape[1]),
        "prefix",
        split_axis=0,
        concat_axis=0,
        tiled=True,
    ).reshape(slots, packed.shape[1])
    attended = merge(pick, back, suffix_sum, suffix_lse)
    return lax.all_to_all(attended, "tensor", split_axis=0, concat_axis=1, tiled=True)


def solution(mesh):
    in_specs = (
        P(("prefix", "tensor"), None),
        P("prefix", None, "tensor", None, None),
        P("prefix"),
        P("prefix", None, "tensor", None, None),
        P("prefix"),
        P(),
    )
    out_specs = P(("prefix", "tensor"), None)
    return jax.shard_map(
        on_device, mesh=mesh, in_specs=in_specs, out_specs=out_specs, check_vma=False
    )
```

```python
import functools
import math

import jax
import jax.numpy as jnp
from jax import lax
from jax.experimental import pallas as pl
from jax.experimental.pallas import tpu as pltpu
from jax.sharding import PartitionSpec as P

H = 64
KVH = 8
HD = 128
LANES = 128
GROUP = H // KVH
LOG2E = 1.4426950408889634
SCALE2 = LOG2E / math.sqrt(HD)
MESH = pl.DeviceIdType.MESH


def nt_dot(a, b):
    return lax.dot_general(a, b, (((1,), (1,)), ((), ())), preferred_element_type=jnp.float32)


def nn_dot(a, b):
    return lax.dot_general(a, b, (((1,), (0,)), ((), ())), preferred_element_type=jnp.float32)


def lane_column(block, lane, index):
    return jnp.sum(jnp.where(lane == index, block, 0.0), axis=1, keepdims=True)


def attend_tile(q, kv_ref, g, chunk):
    length = kv_ref.shape[2]
    top = total = acc = None
    for start in range(0, length, chunk):
        s = nt_dot(q, kv_ref[0, g, start : start + chunk, :]) * SCALE2
        here = jnp.max(s, axis=1, keepdims=True)
        new_top = here if top is None else jnp.maximum(top, here)
        w = jnp.exp2(s - new_top)
        w_sum = jnp.sum(w, axis=1, keepdims=True)
        w_v = nn_dot(w.astype(jnp.bfloat16), kv_ref[1, g, start : start + chunk, :])
        if top is None:
            total, acc = w_sum, w_v
        else:
            fade = jnp.exp2(top - new_top)
            total = total * fade + w_sum
            acc = acc * fade + w_v
        top = new_top
    return acc / total, top + jnp.log(total) * LOG2E


def whole_kernel(
    owners, parts, q_ref, pick_ref, pick_t_ref, len_ref, suffix_hbm, prefix_hbm, out_ref,
    home, home_f, outgoing, arrived, returned, back, lse_out, lse_back, stage, stage_two,
    lse_stage, lse_home, share_p, share_s, suffix_sum, attended, suffix_v, prefix_v,
    bar_home_send, home_recv, out_send, out_recv, ret_send, ret_recv,
    lse_send, lse_recv, att_send, att_recv, own_sem, suffix_sem, prefix_sem,
):
    me = lax.axis_index("prefix")
    me_t = lax.axis_index("tensor")
    kv_heads, _, capacity, wide = outgoing.shape
    part_rows = home.shape[1]
    row_width = home.shape[2]
    rows_home = home_f.shape[0]
    slots = stage.shape[0]
    blocks = suffix_sem.shape[0]
    rows = rows_home // blocks
    count = suffix_v.shape[3]

    def peer(d):
        return lax.rem(me + d, owners)

    def peer_t(d):
        return lax.rem(me_t + d, parts)

    def suffix_copy(b):
        at = pl.ds(b * rows, rows)
        return pltpu.make_async_copy(suffix_hbm.at[at], suffix_v.at[at], suffix_sem.at[b])

    def prefix_copy(g):
        return pltpu.make_async_copy(
            prefix_hbm.at[0, :, g], prefix_v.at[:, g], prefix_sem.at[g]
        )

    for b in range(blocks):
        suffix_copy(b).start()
    for g in range(kv_heads):
        prefix_copy(g).start()

    barrier = pltpu.get_barrier_semaphore()

    def greet(d, carry):
        pl.semaphore_signal(barrier, inc=1, device_id={"prefix": peer(d)}, device_id_type=MESH)
        return carry

    def greet_t(d, carry):
        pl.semaphore_signal(barrier, inc=1, device_id={"tensor": peer_t(d)}, device_id_type=MESH)
        return carry

    lax.fori_loop(1, owners, greet, 0)
    lax.fori_loop(1, parts, greet_t, 0)
    pl.semaphore_wait(barrier, owners + parts - 2)

    def home_copy(d):
        cols = pl.ds(pl.multiple_of(peer_t(d) * row_width, LANES), row_width)
        return pltpu.make_async_remote_copy(
            src_ref=q_ref.at[:, cols], dst_ref=home.at[me_t],
            send_sem=bar_home_send.at[d], recv_sem=home_recv.at[d],
            device_id={"tensor": peer_t(d)}, device_id_type=MESH,
        )

    def exchange(src, dst, send_sem, recv_sem, d):
        return pltpu.make_async_remote_copy(
            src_ref=src, dst_ref=dst, send_sem=send_sem, recv_sem=recv_sem,
            device_id={"prefix": peer(d)}, device_id_type=MESH,
        )

    def out_copy(g, d):
        return exchange(
            outgoing.at[g, peer(d)], arrived.at[g, me], out_send.at[g, d], out_recv.at[g, d], d
        )

    def ret_copy(g, d):
        return exchange(
            returned.at[g, peer(d)], back.at[g, me], ret_send.at[g, d], ret_recv.at[g, d], d
        )

    def lse_copy(d):
        return exchange(lse_out.at[peer(d)], lse_back.at[me], lse_send.at[d], lse_recv.at[d], d)

    def att_copy(g, d):
        cols = pl.ds(pl.multiple_of(me_t * row_width + g * wide, LANES), wide)
        return pltpu.make_async_remote_copy(
            src_ref=attended.at[g, peer_t(d)], dst_ref=out_ref.at[:, cols],
            send_sem=att_send.at[g, d], recv_sem=att_recv.at[g, d],
            device_id={"tensor": peer_t(d)}, device_id_type=MESH,
        )

    def loop(low, high, act):
        def step(i, carry):
            act(i)
            return carry
        lax.fori_loop(low, high, step, 0)

    loop(1, parts, lambda d: home_copy(d).start())
    own_cols = pl.ds(pl.multiple_of(me_t * row_width, LANES), row_width)
    own_home = pltpu.make_async_copy(q_ref.at[:, own_cols], home.at[me_t], own_sem.at[0, 0])
    own_home.start()
    own_home.wait()
    loop(1, parts, lambda d: home_copy(d).wait_recv())
    for t in range(parts):
        home_f[t * part_rows : (t + 1) * part_rows, :] = home[t].astype(jnp.float32)

    def spread(target, g, source):
        for o in range(owners):
            target[g, o] = source[o * capacity : (o + 1) * capacity, :].astype(jnp.bfloat16)

    def gather(target, g, source):
        for o in range(owners):
            target[o * capacity : (o + 1) * capacity, :] = source[g, o].astype(jnp.float32)

    def wide_cols(g):
        return pl.ds(pl.multiple_of(g * wide, LANES), wide)

    def own_out(g):
        return pltpu.make_async_copy(outgoing.at[g, me], arrived.at[g, me], own_sem.at[1, g])

    def own_back(g):
        return pltpu.make_async_copy(returned.at[g, me], back.at[g, me], own_sem.at[2, g])

    def own_att(g):
        cols = pl.ds(pl.multiple_of(me_t * row_width + g * wide, LANES), wide)
        return pltpu.make_async_copy(attended.at[g, me_t], out_ref.at[:, cols], own_sem.at[3, g])

    def dispatch(g):
        stage[...] = nn_dot(pick_t_ref[...], home_f[:, wide_cols(g)].astype(jnp.bfloat16))
        spread(outgoing, g, stage)
        own_out(g).start()
        loop(1, owners, lambda d: out_copy(g, d).start())

    loop(0, kv_heads, dispatch)

    tall = GROUP * rows
    row_of = lax.broadcasted_iota(jnp.int32, (tall, rows * count), 0) % rows
    col = lax.broadcasted_iota(jnp.int32, (tall, rows * count), 1)
    own_block = col // count == row_of
    place = col % count
    row_lane = lax.broadcasted_iota(jnp.int32, (rows, LANES), 1)
    slot_lane = lax.broadcasted_iota(jnp.int32, (slots, LANES), 1)
    home_lane = lax.broadcasted_iota(jnp.int32, (rows_home, LANES), 1)
    lse_stage[...] = jnp.zeros_like(lse_stage)
    lse_home[...] = jnp.zeros_like(lse_home)

    def suffix_block(b):
        suffix_copy(b).wait()
        at = pl.ds(pl.multiple_of(b * rows, rows), rows)
        lengths = jnp.concatenate([len_ref[at, 0:1]] * GROUP, axis=0)
        live = own_block & (place < lengths)

        def suffix_head(g):
            cols = [
                pl.ds(pl.multiple_of((g * GROUP + i) * HD, HD), HD) for i in range(GROUP)
            ]
            q = jnp.concatenate([home_f[at, c] for c in cols], axis=0).astype(jnp.bfloat16)
            keys = suffix_v[at, 0, g].reshape(rows * count, HD)
            values = suffix_v[at, 1, g].reshape(rows * count, HD)
            s = jnp.where(live, nt_dot(q, keys) * SCALE2, -jnp.inf)
            top = jnp.max(s, axis=1, keepdims=True)
            w = jnp.exp2(s - top)
            total = jnp.sum(w, axis=1, keepdims=True)
            part = nn_dot(w.astype(jnp.bfloat16), values) / total
            lse = top + jnp.log(total) * LOG2E
            for i in range(GROUP):
                piece = slice(i * rows, (i + 1) * rows)
                suffix_sum[at, cols[i]] = part[piece]
                lse_home[at, :] = jnp.where(
                    row_lane == g * GROUP + i, lse[piece], lse_home[at, :]
                )

        loop(0, kv_heads, suffix_head)

    loop(0, blocks, suffix_block)

    pair = 2
    chunk = min(1024, prefix_v.shape[2])

    def prefix_head(g):
        own_out(g).wait()
        loop(1, owners, lambda d: out_copy(g, d).wait_recv())
        gather(stage, g, arrived)
        prefix_copy(g).wait()

        def tile(t):
            cols = [pl.ds(pl.multiple_of((t * pair + i) * HD, HD), HD) for i in range(pair)]
            q = jnp.concatenate([stage[:, c] for c in cols], axis=0).astype(jnp.bfloat16)
            part, lse = attend_tile(q, prefix_v, g, chunk)
            for i in range(pair):
                piece = slice(i * slots, (i + 1) * slots)
                stage_two[:, cols[i]] = part[piece]
                lse_stage[...] = jnp.where(
                    slot_lane == g * GROUP + t * pair + i, lse[piece], lse_stage[...]
                )

        loop(0, GROUP // pair, tile)
        spread(returned, g, stage_two)
        own_back(g).start()
        loop(1, owners, lambda d: ret_copy(g, d).start())

    loop(0, kv_heads, prefix_head)

    for o in range(owners):
        lse_out[o] = lse_stage[o * capacity : (o + 1) * capacity, :]
    own_lse = pltpu.make_async_copy(lse_out.at[me], lse_back.at[me], own_sem.at[0, 0])
    own_lse.start()
    loop(1, owners, lambda d: lse_copy(d).start())
    own_lse.wait()
    loop(1, owners, lambda d: lse_copy(d).wait_recv())
    for o in range(owners):
        lse_stage[o * capacity : (o + 1) * capacity, :] = lse_back[o]
    prefix_lse = lax.dot_general(
        pick_ref[...].astype(jnp.float32), lse_stage[...], (((1,), (0,)), ((), ())),
        precision=lax.Precision.HIGHEST, preferred_element_type=jnp.float32,
    )
    suffix_lse = lse_home[...]
    joint = jnp.maximum(prefix_lse, suffix_lse)
    prefix_mass = jnp.exp2(prefix_lse - joint)
    suffix_mass = jnp.exp2(suffix_lse - joint)
    mass = prefix_mass + suffix_mass
    share_p[...] = prefix_mass / mass
    share_s[...] = suffix_mass / mass

    def merge_head(g):
        own_back(g).wait()
        loop(1, owners, lambda d: ret_copy(g, d).wait_recv())
        gather(stage, g, back)
        picked = nn_dot(pick_ref[...], stage[...].astype(jnp.bfloat16))
        for i in range(GROUP):
            head = g * GROUP + i
            from_prefix = lane_column(share_p[...], home_lane, head)
            from_suffix = lane_column(share_s[...], home_lane, head)
            here = pl.ds(pl.multiple_of(head * HD, HD), HD)
            mixed = from_prefix * picked[:, i * HD : (i + 1) * HD]
            mixed = mixed + from_suffix * suffix_sum[:, here]
            for t in range(parts):
                attended[g, t, :, i * HD : (i + 1) * HD] = mixed[
                    t * part_rows : (t + 1) * part_rows
                ].astype(jnp.bfloat16)
        own_att(g).start()
        loop(1, parts, lambda d: att_copy(g, d).start())

    loop(0, kv_heads, merge_head)

    def finish(g):
        own_att(g).wait()
        loop(1, parts, lambda d: att_copy(g, d).wait())
        loop(1, owners, lambda d: out_copy(g, d).wait_send())
        loop(1, owners, lambda d: ret_copy(g, d).wait_send())

    loop(0, kv_heads, finish)
    loop(1, owners, lambda d: lse_copy(d).wait_send())
    loop(1, parts, lambda d: home_copy(d).wait_send())


def on_device(queries, suffix_kv, suffix_lengths, prefix_kv, tree_ids, owner_map):
    owners = lax.axis_size("prefix")
    parts = lax.axis_size("tensor")
    part_rows, full_width = queries.shape
    rows_home, row_width = part_rows * parts, full_width // parts
    kv_heads, count = suffix_kv.shape[2], suffix_kv.shape[3]
    length = prefix_kv.shape[3]
    wide = row_width // kv_heads
    capacity = max(2, 2 * rows_home // owners)
    slots = owners * capacity
    prompts = owner_map.shape[0]
    prompt_iota = jnp.arange(prompts, dtype=jnp.int32)
    prompt_match = tree_ids[:, None] == prompt_iota[None, :]
    owner_row = jnp.sum(jnp.where(prompt_match, owner_map[None, :], 0), axis=1)
    row_iota = jnp.arange(rows_home, dtype=jnp.int32)
    earlier = (tree_ids[:, None] == tree_ids[None, :]) & (row_iota[None, :] < row_iota[:, None])
    slot_rank = jnp.sum(earlier.astype(jnp.int32), axis=1)
    slot_of = owner_row * capacity + slot_rank
    slot_iota = jnp.arange(slots, dtype=jnp.int32)
    pick = (slot_of[:, None] == slot_iota[None, :]).astype(jnp.bfloat16)
    pick_t = (slot_of[None, :] == slot_iota[:, None]).astype(jnp.bfloat16)
    lengths = jnp.broadcast_to(suffix_lengths[:, None], (rows_home, LANES))
    blocks = rows_home // math.gcd(rows_home, 16)
    bf16, f32 = jnp.bfloat16, jnp.float32
    vmem = pl.BlockSpec(memory_space=pltpu.VMEM)
    hbm = pl.BlockSpec(memory_space=pl.ANY)
    dma = pltpu.SemaphoreType.DMA
    slot_block = (kv_heads, owners, capacity, wide)
    return pl.pallas_call(
        functools.partial(whole_kernel, owners, parts),
        out_shape=jax.ShapeDtypeStruct((part_rows, full_width), bf16),
        in_specs=[vmem, vmem, vmem, vmem, hbm, hbm],
        out_specs=vmem,
        scratch_shapes=[
            pltpu.VMEM((parts, part_rows, row_width), bf16),
            pltpu.VMEM((rows_home, row_width), f32),
            pltpu.VMEM(slot_block, bf16),
            pltpu.VMEM(slot_block, bf16),
            pltpu.VMEM(slot_block, bf16),
            pltpu.VMEM(slot_block, bf16),
            pltpu.VMEM((owners, capacity, LANES), f32),
            pltpu.VMEM((owners, capacity, LANES), f32),
            pltpu.VMEM((slots, wide), f32),
            pltpu.VMEM((slots, wide), f32),
            pltpu.VMEM((slots, LANES), f32),
            pltpu.VMEM((rows_home, LANES), f32),
            pltpu.VMEM((rows_home, LANES), f32),
            pltpu.VMEM((rows_home, LANES), f32),
            pltpu.VMEM((rows_home, row_width), f32),
            pltpu.VMEM((kv_heads, parts, part_rows, wide), bf16),
            pltpu.VMEM((rows_home, 2, kv_heads, count, HD), bf16),
            pltpu.VMEM((2, kv_heads, length, HD), bf16),
            dma((parts,)),
            dma((parts,)),
            dma((kv_heads, owners)),
            dma((kv_heads, owners)),
            dma((kv_heads, owners)),
            dma((kv_heads, owners)),
            dma((owners,)),
            dma((owners,)),
            dma((kv_heads, parts)),
            dma((kv_heads, parts)),
            dma((4, kv_heads)),
            dma((blocks,)),
            dma((kv_heads,)),
        ],
        compiler_params=pltpu.CompilerParams(
            collective_id=0, has_side_effects=True, vmem_limit_bytes=56 << 20
        ),
        name="whole_step",
    )(queries, pick, pick_t, lengths, suffix_kv, prefix_kv)


def solution(mesh):
    in_specs = (
        P(("prefix", "tensor"), None),
        P("prefix", None, "tensor", None, None),
        P("prefix"),
        P("prefix", None, "tensor", None, None),
        P("prefix"),
        P(),
    )
    out_specs = P(("prefix", "tensor"), None)
    return jax.shard_map(
        on_device, mesh=mesh, in_specs=in_specs, out_specs=out_specs, check_vma=False
    )
```

```python
import functools
import math

import jax
import jax.numpy as jnp
from jax import lax
from jax.experimental import pallas as pl
from jax.experimental.pallas import tpu as pltpu
from jax.sharding import PartitionSpec as P

H = 64
KVH = 8
HD = 128
LANES = 128
GROUP = H // KVH
LOG2E = 1.4426950408889634
SCALE2 = LOG2E / math.sqrt(HD)
MESH = pl.DeviceIdType.MESH


def nt_dot(a, b):
    return lax.dot_general(a, b, (((1,), (1,)), ((), ())), preferred_element_type=jnp.float32)


def nn_dot(a, b):
    return lax.dot_general(a, b, (((1,), (0,)), ((), ())), preferred_element_type=jnp.float32)


def lane_column(block, lane, index):
    return jnp.sum(jnp.where(lane == index, block, 0.0), axis=1, keepdims=True)


def attend_tile(q, kv_ref, g, chunk):
    length = kv_ref.shape[2]
    top = total = acc = None
    for start in range(0, length, chunk):
        s = nt_dot(q, kv_ref[0, g, start : start + chunk, :]) * SCALE2
        here = jnp.max(s, axis=1, keepdims=True)
        new_top = here if top is None else jnp.maximum(top, here)
        w = jnp.exp2(s - new_top)
        w_sum = jnp.sum(w, axis=1, keepdims=True)
        w_v = nn_dot(w.astype(jnp.bfloat16), kv_ref[1, g, start : start + chunk, :])
        if top is None:
            total, acc = w_sum, w_v
        else:
            fade = jnp.exp2(top - new_top)
            total = total * fade + w_sum
            acc = acc * fade + w_v
        top = new_top
    return acc / total, top + jnp.log(total) * LOG2E


def whole_kernel(
    owners, parts, q_ref, tree_ref, len_ref, map_ref, suffix_hbm, prefix_hbm, out_ref,
    pick_ref, pick_t_ref, home, home_f, outgoing, arrived, returned, back, lse_out, lse_back, stage, stage_two,
    lse_stage, lse_in, lse_home, share_p, share_s, suffix_sum, attended, suffix_v, prefix_v,
    len_all,
    bar_home_send, home_recv, out_send, out_recv, ret_send, ret_recv,
    lse_send, lse_recv, att_send, att_recv, own_sem, suffix_sem, prefix_sem,
):
    me = lax.axis_index("prefix")
    me_t = lax.axis_index("tensor")
    kv_heads, _, capacity, wide = outgoing.shape
    part_rows = home.shape[2]
    row_width = home_f.shape[1]
    rows_home = home_f.shape[0]
    slots = stage.shape[0]
    blocks = suffix_sem.shape[0]
    rows = rows_home // blocks
    count = suffix_v.shape[3]

    def peer(d):
        return lax.rem(me + d, owners)

    def peer_t(d):
        return lax.rem(me_t + d, parts)

    def suffix_copy(b):
        at = pl.ds(b * rows, rows)
        return pltpu.make_async_copy(suffix_hbm.at[at], suffix_v.at[at], suffix_sem.at[b])

    def prefix_copy(g):
        return pltpu.make_async_copy(
            prefix_hbm.at[0, :, g], prefix_v.at[:, g], prefix_sem.at[g]
        )

    for b in range(blocks):
        suffix_copy(b).start()
    for g in range(kv_heads):
        prefix_copy(g).start()

    barrier = pltpu.get_barrier_semaphore()

    def greet(d, carry):
        pl.semaphore_signal(barrier, inc=1, device_id={"prefix": peer(d)}, device_id_type=MESH)
        return carry

    def greet_t(d, carry):
        pl.semaphore_signal(barrier, inc=1, device_id={"tensor": peer_t(d)}, device_id_type=MESH)
        return carry

    lax.fori_loop(1, owners, greet, 0)
    lax.fori_loop(1, parts, greet_t, 0)
    pl.semaphore_wait(barrier, owners + parts - 2)

    def home_copy(g, d):
        cols = pl.ds(pl.multiple_of(peer_t(d) * row_width + g * wide, LANES), wide)
        return pltpu.make_async_remote_copy(
            src_ref=q_ref.at[:, cols], dst_ref=home.at[g, me_t],
            send_sem=bar_home_send.at[g, d], recv_sem=home_recv.at[g, d],
            device_id={"tensor": peer_t(d)}, device_id_type=MESH,
        )

    def exchange(src, dst, send_sem, recv_sem, d):
        return pltpu.make_async_remote_copy(
            src_ref=src, dst_ref=dst, send_sem=send_sem, recv_sem=recv_sem,
            device_id={"prefix": peer(d)}, device_id_type=MESH,
        )

    def out_copy(g, d):
        return exchange(
            outgoing.at[g, peer(d)], arrived.at[g, me], out_send.at[g, d], out_recv.at[g, d], d
        )

    def ret_copy(g, d):
        return exchange(
            returned.at[g, peer(d)], back.at[g, me], ret_send.at[g, d], ret_recv.at[g, d], d
        )

    def lse_copy(g, d):
        return exchange(
            lse_out.at[g, peer(d)], lse_back.at[g, me], lse_send.at[g, d], lse_recv.at[g, d], d
        )

    def own_lse(g):
        return pltpu.make_async_copy(lse_out.at[g, me], lse_back.at[g, me], own_sem.at[4, g])

    def att_copy(g, d):
        cols = pl.ds(pl.multiple_of(me_t * row_width + g * wide, LANES), wide)
        return pltpu.make_async_remote_copy(
            src_ref=attended.at[g, peer_t(d)], dst_ref=out_ref.at[:, cols],
            send_sem=att_send.at[g, d], recv_sem=att_recv.at[g, d],
            device_id={"tensor": peer_t(d)}, device_id_type=MESH,
        )

    def loop(low, high, act):
        def step(i, carry):
            act(i)
            return carry
        lax.fori_loop(low, high, step, 0)

    def own_home(g):
        cols = pl.ds(pl.multiple_of(me_t * row_width + g * wide, LANES), wide)
        return pltpu.make_async_copy(q_ref.at[:, cols], home.at[g, me_t], own_sem.at[0, g])

    def start_home(g):
        loop(1, parts, lambda d: home_copy(g, d).start())
        own_home(g).start()

    loop(0, kv_heads, start_home)

    f32 = jnp.float32
    prompts = map_ref.shape[1]
    row_at = lax.broadcasted_iota(jnp.int32, (rows_home, rows_home), 0)
    col_at = lax.broadcasted_iota(jnp.int32, (rows_home, rows_home), 1)
    on_diagonal = row_at == col_at

    def as_column(row_vector):
        spread_rows = jnp.broadcast_to(row_vector, (rows_home, rows_home))
        return jnp.sum(jnp.where(on_diagonal, spread_rows, 0.0), axis=1, keepdims=True)

    tree_row = tree_ref[...].astype(f32)
    tree_col = as_column(tree_row)
    len_col = as_column(len_ref[...].astype(f32)).astype(jnp.int32)
    earlier = (tree_col == tree_row) & (col_at < row_at)
    rank = jnp.sum(jnp.where(earlier, 1.0, 0.0), axis=1, keepdims=True)
    prompt_at = lax.broadcasted_iota(jnp.int32, (rows_home, prompts), 1).astype(f32)
    owner_of = jnp.sum(
        jnp.where(prompt_at == tree_col, map_ref[...].astype(f32), 0.0), axis=1, keepdims=True
    )
    slot_of = owner_of * capacity + rank
    slot_at = lax.broadcasted_iota(jnp.int32, (rows_home, slots), 1).astype(f32)
    pick = jnp.where(slot_of == slot_at, 1.0, 0.0)
    pick_ref[...] = pick.astype(jnp.bfloat16)
    pick_t_ref[...] = pick.T.astype(jnp.bfloat16)
    len_wide = jnp.broadcast_to(len_col, (rows_home, LANES))
    len_all[...] = len_wide

    def spread(target, g, source):
        for o in range(owners):
            target[g, o] = source[o * capacity : (o + 1) * capacity, :].astype(jnp.bfloat16)

    def gather(target, g, source):
        for o in range(owners):
            target[o * capacity : (o + 1) * capacity, :] = source[g, o].astype(jnp.float32)

    def wide_cols(g):
        return pl.ds(pl.multiple_of(g * wide, LANES), wide)

    def own_out(g):
        return pltpu.make_async_copy(outgoing.at[g, me], arrived.at[g, me], own_sem.at[1, g])

    def own_back(g):
        return pltpu.make_async_copy(returned.at[g, me], back.at[g, me], own_sem.at[2, g])

    def own_att(g):
        cols = pl.ds(pl.multiple_of(me_t * row_width + g * wide, LANES), wide)
        return pltpu.make_async_copy(attended.at[g, me_t], out_ref.at[:, cols], own_sem.at[3, g])

    def dispatch(g):
        own_home(g).wait()
        loop(1, parts, lambda d: home_copy(g, d).wait_recv())
        for t in range(parts):
            home_f[t * part_rows : (t + 1) * part_rows, wide_cols(g)] = home[g, t].astype(f32)
        stage[...] = nn_dot(pick_t_ref[...], home_f[:, wide_cols(g)].astype(jnp.bfloat16))
        spread(outgoing, g, stage)
        own_out(g).start()
        loop(1, owners, lambda d: out_copy(g, d).start())

    loop(0, kv_heads, dispatch)

    tall = GROUP * rows
    row_of = lax.broadcasted_iota(jnp.int32, (tall, rows * count), 0) % rows
    col = lax.broadcasted_iota(jnp.int32, (tall, rows * count), 1)
    own_block = col // count == row_of
    place = col % count
    row_lane = lax.broadcasted_iota(jnp.int32, (rows, LANES), 1)
    slot_lane = lax.broadcasted_iota(jnp.int32, (slots, LANES), 1)
    home_lane = lax.broadcasted_iota(jnp.int32, (rows_home, LANES), 1)
    lse_stage[...] = jnp.zeros_like(lse_stage)
    lse_home[...] = jnp.zeros_like(lse_home)

    def suffix_block(b):
        suffix_copy(b).wait()
        at = pl.ds(pl.multiple_of(b * rows, rows), rows)
        lengths = jnp.concatenate([len_all[at, 0:1]] * GROUP, axis=0)
        live = own_block & (place < lengths)

        def suffix_head(g):
            cols = [
                pl.ds(pl.multiple_of((g * GROUP + i) * HD, HD), HD) for i in range(GROUP)
            ]
            q = jnp.concatenate([home_f[at, c] for c in cols], axis=0).astype(jnp.bfloat16)
            keys = suffix_v[at, 0, g].reshape(rows * count, HD)
            values = suffix_v[at, 1, g].reshape(rows * count, HD)
            s = jnp.where(live, nt_dot(q, keys) * SCALE2, -jnp.inf)
            top = jnp.max(s, axis=1, keepdims=True)
            w = jnp.exp2(s - top)
            total = jnp.sum(w, axis=1, keepdims=True)
            part = nn_dot(w.astype(jnp.bfloat16), values) / total
            lse = top + jnp.log(total) * LOG2E
            for i in range(GROUP):
                piece = slice(i * rows, (i + 1) * rows)
                suffix_sum[at, cols[i]] = part[piece]
                lse_home[at, :] = jnp.where(
                    row_lane == g * GROUP + i, lse[piece], lse_home[at, :]
                )

        loop(0, kv_heads, suffix_head)

    loop(0, blocks, suffix_block)

    pair = 4
    chunk = min(1024, prefix_v.shape[2])

    def prefix_head(g):
        own_out(g).wait()
        loop(1, owners, lambda d: out_copy(g, d).wait_recv())
        gather(stage, g, arrived)
        prefix_copy(g).wait()

        def tile(t):
            cols = [pl.ds(pl.multiple_of((t * pair + i) * HD, HD), HD) for i in range(pair)]
            q = jnp.concatenate([stage[:, c] for c in cols], axis=0).astype(jnp.bfloat16)
            part, lse = attend_tile(q, prefix_v, g, chunk)
            for i in range(pair):
                piece = slice(i * slots, (i + 1) * slots)
                stage_two[:, cols[i]] = part[piece]
                lse_stage[...] = jnp.where(
                    slot_lane == g * GROUP + t * pair + i, lse[piece], lse_stage[...]
                )

        loop(0, GROUP // pair, tile)
        for o in range(owners):
            lse_out[g, o] = lse_stage[o * capacity : (o + 1) * capacity, :]
        own_lse(g).start()
        loop(1, owners, lambda d: lse_copy(g, d).start())
        spread(returned, g, stage_two)
        own_back(g).start()
        loop(1, owners, lambda d: ret_copy(g, d).start())

    def merge_head(g):
        own_lse(g).wait()
        loop(1, owners, lambda d: lse_copy(g, d).wait_recv())
        for o in range(owners):
            lse_in[o * capacity : (o + 1) * capacity, :] = lse_back[g, o]
        prefix_lse = lax.dot_general(
            pick_ref[...].astype(f32), lse_in[...], (((1,), (0,)), ((), ())),
            precision=lax.Precision.HIGHEST, preferred_element_type=f32,
        )
        suffix_lse = lse_home[...]
        joint = jnp.maximum(prefix_lse, suffix_lse)
        prefix_mass = jnp.exp2(prefix_lse - joint)
        suffix_mass = jnp.exp2(suffix_lse - joint)
        mass = prefix_mass + suffix_mass
        share_p[...] = prefix_mass / mass
        share_s[...] = suffix_mass / mass
        own_back(g).wait()
        loop(1, owners, lambda d: ret_copy(g, d).wait_recv())
        gather(stage, g, back)
        picked = nn_dot(pick_ref[...], stage[...].astype(jnp.bfloat16))
        for i in range(GROUP):
            head = g * GROUP + i
            from_prefix = lane_column(share_p[...], home_lane, head)
            from_suffix = lane_column(share_s[...], home_lane, head)
            here = pl.ds(pl.multiple_of(head * HD, HD), HD)
            mixed = from_prefix * picked[:, i * HD : (i + 1) * HD]
            mixed = mixed + from_suffix * suffix_sum[:, here]
            for t in range(parts):
                attended[g, t, :, i * HD : (i + 1) * HD] = mixed[
                    t * part_rows : (t + 1) * part_rows
                ].astype(jnp.bfloat16)
        own_att(g).start()
        loop(1, parts, lambda d: att_copy(g, d).start())

    def head_step(g):
        prefix_head(g)
        merge_head(g - 1)

    prefix_head(0)
    loop(1, kv_heads, head_step)
    merge_head(kv_heads - 1)

    def finish(g):
        own_att(g).wait()
        loop(1, parts, lambda d: att_copy(g, d).wait())
        loop(1, owners, lambda d: out_copy(g, d).wait_send())
        loop(1, owners, lambda d: ret_copy(g, d).wait_send())
        loop(1, owners, lambda d: lse_copy(g, d).wait_send())
        loop(1, parts, lambda d: home_copy(g, d).wait_send())

    loop(0, kv_heads, finish)


def on_device(queries, suffix_kv, suffix_lengths, prefix_kv, tree_ids, owner_map):
    owners = lax.axis_size("prefix")
    parts = lax.axis_size("tensor")
    part_rows, full_width = queries.shape
    rows_home, row_width = part_rows * parts, full_width // parts
    kv_heads, count = suffix_kv.shape[2], suffix_kv.shape[3]
    length = prefix_kv.shape[3]
    wide = row_width // kv_heads
    capacity = max(2, 2 * rows_home // owners)
    slots = owners * capacity
    prompts = owner_map.shape[0]
    blocks = rows_home // math.gcd(rows_home, 16)
    bf16, f32 = jnp.bfloat16, jnp.float32
    vmem = pl.BlockSpec(memory_space=pltpu.VMEM)
    hbm = pl.BlockSpec(memory_space=pl.ANY)
    dma = pltpu.SemaphoreType.DMA
    slot_block = (kv_heads, owners, capacity, wide)
    return pl.pallas_call(
        functools.partial(whole_kernel, owners, parts),
        out_shape=jax.ShapeDtypeStruct((part_rows, full_width), bf16),
        in_specs=[vmem, vmem, vmem, vmem, hbm, hbm],
        out_specs=vmem,
        scratch_shapes=[
            pltpu.VMEM((rows_home, slots), bf16),
            pltpu.VMEM((slots, rows_home), bf16),
            pltpu.VMEM((kv_heads, parts, part_rows, wide), bf16),
            pltpu.VMEM((rows_home, row_width), f32),
            pltpu.VMEM(slot_block, bf16),
            pltpu.VMEM(slot_block, bf16),
            pltpu.VMEM(slot_block, bf16),
            pltpu.VMEM(slot_block, bf16),
            pltpu.VMEM((kv_heads, owners, capacity, LANES), f32),
            pltpu.VMEM((kv_heads, owners, capacity, LANES), f32),
            pltpu.VMEM((slots, wide), f32),
            pltpu.VMEM((slots, wide), f32),
            pltpu.VMEM((slots, LANES), f32),
            pltpu.VMEM((slots, LANES), f32),
            pltpu.VMEM((rows_home, LANES), f32),
            pltpu.VMEM((rows_home, LANES), f32),
            pltpu.VMEM((rows_home, LANES), f32),
            pltpu.VMEM((rows_home, row_width), f32),
            pltpu.VMEM((kv_heads, parts, part_rows, wide), bf16),
            pltpu.VMEM((rows_home, 2, kv_heads, count, HD), bf16),
            pltpu.VMEM((2, kv_heads, length, HD), bf16),
            pltpu.VMEM((rows_home, LANES), jnp.int32),
            dma((kv_heads, parts)),
            dma((kv_heads, parts)),
            dma((kv_heads, owners)),
            dma((kv_heads, owners)),
            dma((kv_heads, owners)),
            dma((kv_heads, owners)),
            dma((kv_heads, owners)),
            dma((kv_heads, owners)),
            dma((kv_heads, parts)),
            dma((kv_heads, parts)),
            dma((5, kv_heads)),
            dma((blocks,)),
            dma((kv_heads,)),
        ],
        compiler_params=pltpu.CompilerParams(
            collective_id=0, has_side_effects=True, vmem_limit_bytes=56 << 20
        ),
        name="whole_step",
    )(
        queries,
        tree_ids.reshape(1, rows_home),
        suffix_lengths.reshape(1, rows_home),
        owner_map.reshape(1, prompts),
        suffix_kv,
        prefix_kv,
    )


def solution(mesh):
    in_specs = (
        P(("prefix", "tensor"), None),
        P("prefix", None, "tensor", None, None),
        P("prefix"),
        P("prefix", None, "tensor", None, None),
        P("prefix"),
        P(),
    )
    out_specs = P(("prefix", "tensor"), None)
    return jax.shard_map(
        on_device, mesh=mesh, in_specs=in_specs, out_specs=out_specs, check_vma=False
    )
```
